32 devices in a mesh: groups: 2 (over x), label: 8 (over z, y), cent: 2 (over core).
Axes of the slice: x: 2, y: 2, z: 4, core: 2. Of those that a mesh axis runs over, the one named last changes fastest.
Arguments:
- embeddings: bfloat16 [768, 16384], P('label', 'groups'), parts along dimension 1, may hold values from -40 to 40
- centroids: bfloat16 [2, 8192, 768], P('cent', ('groups', 'label')), parts along dimension 1, may hold values from -1 to 1
Outputs:
- new_centroids: float32 [2, 8192, 768], P('cent', ('groups', 'label')), parts along dimension 1
The draws below stay inside these ranges and needn't reach their ends.
There are 2 independent parts, one for each index of `groups`. The reference program is written for one: setup_inputs(seed, part) draws one part's arguments, and reference() takes and returns one part's arrays. A program takes and returns all parts, laid end to end along the dimension named above; each array names one. Nothing has to cross between parts.
All inputs are finite; a program needn't handle non-finite values.
Results may differ from the reference program's by a relative error of at most 0.012.
Values may be sent and summed in bfloat16 or wider, within the bound.
A program may use at most 128 MiB of HBM per device.

```python
import math
import jax
import jax.numpy as jnp
from jax import lax

D = 768
K = 8192
LAB_DEV = 1024
LABELS = 8192
N_LABEL = 8
N_CENT = 2


def centroid_setup(key):
    centroid_key = jax.random.fold_in(key, 3)
    normals = jnp.clip(jax.random.normal(jax.random.fold_in(centroid_key, 1), (K, D), jnp.float32), -6.0, 6.0)
    row_scale = 0.05 * jnp.exp(jax.random.uniform(jax.random.fold_in(centroid_key, 2), (K, 1), jnp.float32, math.log(0.5), math.log(2.0)))
    centroid_table = normals * row_scale
    return centroid_table


def draw_centroids(key, part):
    centroid_table = centroid_setup(key)
    return centroid_table.reshape(N_CENT, K // N_CENT, D).astype(jnp.bfloat16)


def draw_embeddings(key, part):
    label_key = jax.random.fold_in(key, 5)
    normals = jnp.clip(jax.random.normal(jax.random.fold_in(label_key, 1), (LABELS, D), jnp.float32), -6.0, 6.0)
    row_scale = jnp.exp(jax.random.uniform(jax.random.fold_in(label_key, 2), (LABELS, 1), jnp.float32, math.log(0.5), math.log(2.0)))
    label_table = normals * row_scale
    return label_table.T.astype(jnp.bfloat16)


def setup_inputs(seed: int = 0, part: int = 0) -> dict:
    seeds = jax.random.split(jax.random.key(seed), 3)
    part_keys = jax.random.split(jax.random.fold_in(seeds[2], part), 3)
    embeddings = draw_embeddings(jax.random.fold_in(jax.random.fold_in(seeds[2], part), 71), part)
    centroids = draw_centroids(jax.random.fold_in(jax.random.fold_in(seeds[2], part), 71), part)
    return {"embeddings": embeddings, "centroids": centroids}


prior_weight = 1.0


def reference(embeddings, centroids):
    centroid_table = centroids.reshape(K, D)
    half_norms = 0.5 * jnp.sum(jnp.square(centroid_table.astype(jnp.float32)), axis=1)
    block_rows = math.gcd(LAB_DEV, 512)
    device_blocks = embeddings.T.reshape(N_LABEL, LAB_DEV // block_rows, block_rows, D)

    def absorb(state_pair, piece_rows):
        numerators, counts = state_pair
        scores = jnp.dot(piece_rows, centroid_table.T, preferred_element_type=jnp.float32) - half_norms[None, :]
        row_top = jnp.max(scores, axis=1, keepdims=True)
        exponent = jnp.exp(scores - row_top)
        row_sum = jnp.sum(exponent, axis=1, keepdims=True)
        weights = (exponent / row_sum).astype(jnp.bfloat16)
        numerators = numerators + jnp.dot(weights.T, piece_rows, preferred_element_type=jnp.float32)
        counts = counts + jnp.sum(weights, axis=0, dtype=jnp.float32)
        return (numerators, counts), None

    def device_pass(state_pair, block_pieces):
        start_pair = (jnp.zeros((K, D), jnp.float32), jnp.zeros((K,), jnp.float32))
        (block_sums, block_counts), _ = lax.scan(absorb, start_pair, block_pieces)
        rounded_sums = lax.optimization_barrier(block_sums.astype(jnp.bfloat16))
        rounded_counts = lax.optimization_barrier(block_counts.astype(jnp.bfloat16))
        total_sums = state_pair[0] + rounded_sums.astype(jnp.float32)
        total_counts = state_pair[1] + rounded_counts.astype(jnp.float32)
        return (total_sums, total_counts), None

    first_pair = (jnp.zeros((K, D), jnp.float32), jnp.zeros((K,), jnp.float32))
    (numerators, counts), _ = lax.scan(device_pass, first_pair, device_blocks)
    updated = (numerators + prior_weight * centroid_table.astype(jnp.float32)) / (counts + prior_weight)[:, None]
    return updated.reshape(N_CENT, K // N_CENT, D)
```

```python
import functools
import jax
import jax.numpy as jnp
from jax import lax
from jax.experimental import pallas as pl
from jax.experimental.pallas import tpu as pltpu
from jax.sharding import PartitionSpec as P

prior_weight = 1.0
COLS = 2
CHUNK = 1024
LAG = 1
WAIT = 2
SLOTS = WAIT + 1
MESH = pl.DeviceIdType.MESH


def plain_body(embeddings, centroids):
    held = centroids[0]
    half = embeddings.shape[1] // lax.axis_size("cent")
    mine = lax.dynamic_slice_in_dim(embeddings, lax.axis_index("cent") * half, half, axis=1)
    column = lax.all_gather(mine, "label", axis=0, tiled=True)
    table = lax.all_gather(column, "cent", axis=1, tiled=True)
    half_norms = 0.5 * jnp.sum(jnp.square(held.astype(jnp.float32)), axis=1)
    scores = jnp.dot(held, table, preferred_element_type=jnp.float32) - half_norms[:, None]
    top = jnp.max(scores, axis=0)
    total = jnp.sum(jnp.exp(scores - top[None, :]), axis=0)
    tops = lax.all_gather(jnp.stack([top, total]), ("label", "cent"))
    row_top = jnp.max(tops[:, 0], axis=0)
    row_sum = jnp.sum(tops[:, 1] * jnp.exp(tops[:, 0] - row_top[None]), axis=0)
    weights = (jnp.exp(scores - row_top[None, :]) / row_sum[None, :]).astype(jnp.bfloat16)
    sums = lax.dot_general(weights, table, (((1,), (1,)), ((), ())), preferred_element_type=jnp.float32)
    counts = jnp.sum(weights, axis=1, dtype=jnp.float32)
    updated = (sums + prior_weight * held.astype(jnp.float32)) / (counts + prior_weight)[:, None]
    return updated[None]


def merge(values):
    top = functools.reduce(jnp.maximum, values)
    return top + jnp.log(sum(jnp.exp(value - top) for value in values))


def kernel(n_label, e_ref, c_hbm, out_ref, c_ref, table, expo, tops, stat_core, stat_chip, stat_full, stat_last,
           sums, counts, norms, load_sem, c_sem, send_sem, recv_sem, sib_sem, stat_send, stat_recv, last_send, last_recv):
    rows = e_ref.shape[0]
    labels = table.shape[1]
    width = expo.shape[2]
    chunks = labels // width
    half = width // 2
    n_z = n_label // COLS
    me = lax.axis_index("label")
    core = lax.axis_index("cent")
    z, y = me // COLS, me % COLS
    across_label = z * COLS + 1 - y
    last = chunks - 1

    def block(index):
        return pl.ds(pl.multiple_of(index * rows, rows), rows)

    def columns(j):
        return pl.ds(pl.multiple_of(j * width, width), width)

    def own_half(j):
        return pl.ds(pl.multiple_of(j * width + core * half, half), half)

    load = pltpu.make_async_copy(e_ref, table.at[block(me), :], load_sem)
    load.start()
    c_load = pltpu.make_async_copy(c_hbm, c_ref, c_sem)
    c_load.start()

    barrier = pltpu.get_barrier_semaphore()
    pl.semaphore_signal(barrier, inc=1, device_id={"cent": 1 - core}, device_id_type=MESH)
    pl.semaphore_signal(barrier, inc=1, device_id={"label": across_label}, device_id_type=MESH)

    @pl.when(z < n_z - 1)
    def _():
        pl.semaphore_signal(barrier, inc=1, device_id={"label": me + COLS}, device_id_type=MESH)

    @pl.when(z > 0)
    def _():
        pl.semaphore_signal(barrier, inc=1, device_id={"label": me - COLS}, device_id_type=MESH)

    sums[...] = jnp.zeros_like(sums)
    counts[...] = jnp.zeros_like(counts)
    load.wait()
    pl.semaphore_wait(barrier, 2 + jnp.where(z < n_z - 1, 1, 0) + jnp.where(z > 0, 1, 0))

    def hop(j, index, kind, target):
        part = table.at[block(index), own_half(j)]
        return pltpu.make_async_remote_copy(
            src_ref=part, dst_ref=part, send_sem=send_sem.at[kind],
            recv_sem=recv_sem.at[j, index], device_id={"label": target}, device_id_type=MESH)

    def sibling(j, index, size):
        part = table.at[pl.ds(pl.multiple_of(index * rows, rows), size * rows), own_half(j)]
        return pltpu.make_async_remote_copy(
            src_ref=part, dst_ref=part, send_sem=send_sem.at[3],
            recv_sem=sib_sem.at[j], device_id={"cent": 1 - core}, device_id_type=MESH)

    def up(j, index):
        @pl.when(z < n_z - 1)
        def _():
            hop(j, index, 0, me + COLS).start()

    def down(j, index):
        @pl.when(z > 0)
        def _():
            hop(j, index, 1, me - COLS).start()

    def across(j, index):
        hop(j, index, 2, across_label).start()

    def live(j):
        return jnp.logical_and(j >= 0, j < chunks)

    def relay_own(t):
        @pl.when(t < chunks)
        def _():
            up(t, me)
            down(t, me)
            across(t, me)

    def relay_column(t, d):
        j = t - LAG * d
        for sign in (-1, 1):
            far = z + sign * d
            edge = jnp.logical_or(far == 0, far == n_z - 1)

            @pl.when(live(j) & (far >= 0) & (far < n_z))
            def _():
                index = far * COLS + y
                hop(j, index, 0, me).wait_recv()
                (up if sign < 0 else down)(j, index)

                @pl.when(jnp.logical_not(edge & (j % 2 == 0)))
                def _():
                    across(j, index)

    def relay_across(t, d):
        j = t - LAG * (d + 1)
        for sign in ((1,) if d == 0 else (-1, 1)):
            far = z + sign * d

            @pl.when(live(j) & (far >= 0) & (far < n_z))
            def _():
                index = far * COLS + 1 - y
                hop(j, index, 0, me).wait_recv()

                @pl.when((j % 2 == 0) & (far == 0))
                def _():
                    up(j, index)

                @pl.when((j % 2 == 0) & (far == n_z - 1))
                def _():
                    down(j, index)

                if d == 0:
                    sibling(j, index, 1).start()
                else:
                    sibling(j, far * COLS, COLS).start()

    def tell(part, stage, j, target):
        pltpu.make_async_remote_copy(
            src_ref=part, dst_ref=part, send_sem=stat_send.at[stage],
            recv_sem=stat_recv.at[stage, j], device_id=target, device_id_type=MESH).start()

    def hear(part, stage, j):
        pltpu.make_async_copy(part, part, stat_recv.at[stage, j]).wait()

    def score(j):
        others = table.at[pl.ds(0, (n_label - 1) * rows), pl.ds(0, half)]
        pltpu.make_async_copy(others, others, sib_sem.at[j]).wait()
        products = jnp.dot(c_ref[...], table[:, columns(j)], preferred_element_type=jnp.float32)
        scores = products - norms[:, 0:1]
        top = jnp.max(scores, axis=0, keepdims=True)
        exponent = jnp.exp(scores - top)
        slot = lax.rem(j, SLOTS)
        expo[slot] = exponent
        tops[slot] = top
        level = top + jnp.log(jnp.sum(exponent, axis=0, keepdims=True))
        stat_core[j, core, 0] = level[:, :half]
        stat_core[j, core, 1] = level[:, half:]

    def tell_core(j):
        tell(stat_core.at[j, core, 1 - core], 0, j, {"cent": 1 - core})

    def join_cores(j):
        hear(stat_core.at[j, 0, 0], 0, j)
        stat_chip[j, me] = merge([stat_core[j, 0, core], stat_core[j, 1, core]])
        for k in range(1, n_label):
            tell(stat_chip.at[j, me], 1, j, {"label": lax.rem(me + k, n_label)})

    def join_chips(j):
        hear(stat_chip.at[j, pl.ds(0, n_label - 1)], 1, j)
        stat_full[j, core] = merge([stat_chip[j, k] for k in range(n_label)])
        tell(stat_full.at[j, core], 2, j, {"cent": 1 - core})

    def weigh(j, level):
        slot = lax.rem(j, SLOTS)
        factor = jnp.exp(tops[slot] - level)
        weights = (expo[slot] * factor).astype(jnp.bfloat16)
        gained = lax.dot_general(
            weights, table[:, columns(j)], (((1,), (1,)), ((), ())), preferred_element_type=jnp.float32)
        part = counts[...]
        for k in range(width // 128):
            part += weights[:, k * 128:(k + 1) * 128].astype(jnp.float32)
        return gained, part

    def absorb(j):
        hear(stat_full.at[j, 0], 2, j)
        level = jnp.concatenate([stat_full[j, 0], stat_full[j, 1]], axis=1)
        gained, part = weigh(j, level)
        sums[...] += gained
        counts[...] = part

    def when_live(j, step):
        @pl.when(jnp.logical_and(j >= 0, j < last))
        def _():
            step(j)

    def relays(t, part):
        if part == 0:
            relay_own(t)
        for d in ((1,), (2,), range(3, n_z))[part]:
            relay_column(t, d)
            relay_across(t, d - 1)
        if part == 2:
            relay_across(t, n_z - 1)

    def tick(t, carry):
        scored = t - LAG * n_z - 1
        when_live(scored - WAIT, join_chips)
        relays(t, 0)

        @pl.when(t == 0)
        def _():
            c_load.wait()
            centroids = c_ref[...].astype(jnp.float32)
            norms[...] = jnp.broadcast_to(0.5 * jnp.sum(centroids * centroids, axis=1, keepdims=True), norms.shape)

        @pl.when(live(scored))
        def _():
            score(scored)
            tell_core(scored)

        relays(t, 1)
        when_live(scored - WAIT, absorb)
        when_live(scored, join_cores)
        relays(t, 2)
        return carry

    final = last + LAG * n_z
    lax.fori_loop(0, final, tick, 0)

    def score_full(j):
        score(j)
        tell_core(j)

    scored = last - 1
    join_chips(scored - WAIT)
    relays(jnp.int32(final), 0)
    relays(jnp.int32(final), 1)
    score(scored)
    tell_core(scored)
    absorb(scored - WAIT)
    join_cores(scored)
    relays(jnp.int32(final), 2)
    score(last)
    tell(stat_core.at[last, core], 0, last, {"cent": 1 - core})
    for j in range(scored - WAIT + 1, last):
        join_chips(j)
    absorb(scored - WAIT + 1)
    hear(stat_core.at[last, 0], 0, last)
    for k in range(2):
        stat_last[me, k] = merge([stat_core[last, 0, k], stat_core[last, 1, k]])
    for k in range(1, n_label):
        pltpu.make_async_remote_copy(
            src_ref=stat_last.at[me], dst_ref=stat_last.at[me], send_sem=last_send, recv_sem=last_recv,
            device_id={"label": lax.rem(me + k, n_label)}, device_id_type=MESH).start()
    for j in range(scored - WAIT + 2, last):
        absorb(j)
    heard = stat_last.at[pl.ds(0, n_label - 1)]
    pltpu.make_async_copy(heard, heard, last_recv).wait()
    level = jnp.concatenate([merge([stat_last[i, k] for i in range(n_label)]) for k in range(2)], axis=1)
    gained, part = weigh(last, level)
    total = jnp.sum(part, axis=1, keepdims=True)
    out_ref[...] = (sums[...] + gained + prior_weight * c_ref[...].astype(jnp.float32)) * (1.0 / (total + prior_weight))

    def drain(kind, halves):
        ref = table.at[pl.ds(0, halves * rows // 2), pl.ds(0, labels // 2)]
        pltpu.make_async_copy(ref, ref, send_sem.at[kind]).wait()

    for k in range(n_z):
        @pl.when(z == k)
        def _():
            if k < n_z - 1:
                drain(0, 2 * (k + 1) + 1)
            if k > 0:
                drain(1, 2 * (n_z - k) + 1)
            drain(2, 2 * n_z - (1 if k in (0, n_z - 1) else 2))
    drain(3, 2 * (n_label - 1))
    pltpu.make_async_copy(heard, heard, last_send).wait()
    told = (stat_core.at[:, 0, 0], stat_chip.at[pl.ds(0, last), pl.ds(0, n_label - 1)], stat_full.at[pl.ds(0, last), 0])
    for stage, part in enumerate(told):
        pltpu.make_async_copy(part, part, stat_send.at[stage]).wait()
    pltpu.make_async_copy(stat_core.at[0, 0, 0], stat_core.at[0, 0, 0], stat_send.at[0]).wait()


def fused_body(n_label, embeddings, centroids):
    held = centroids[0]
    rows, labels = embeddings.shape
    count, depth = held.shape
    chunks = labels // CHUNK
    half = CHUNK // 2
    updated = pl.pallas_call(
        functools.partial(kernel, n_label),
        out_shape=pltpu.VMEM((count, depth), jnp.float32),
        in_specs=[pl.BlockSpec(memory_space=pl.ANY)] * 2,
        out_specs=pl.BlockSpec(memory_space=pltpu.VMEM),
        scratch_shapes=[
            pltpu.VMEM((count, depth), jnp.bfloat16),
            pltpu.VMEM((depth, labels), jnp.bfloat16),
            pltpu.VMEM((SLOTS, count, CHUNK), jnp.float32),
            pltpu.VMEM((SLOTS, 1, CHUNK), jnp.float32),
            pltpu.VMEM((chunks, 2, 2, 1, half), jnp.float32),
            pltpu.VMEM((chunks, n_label, 1, half), jnp.float32),
            pltpu.VMEM((chunks, 2, 1, half), jnp.float32),
            pltpu.VMEM((n_label, 2, 1, half), jnp.float32),
            pltpu.VMEM((count, depth), jnp.float32),
            pltpu.VMEM((count, 128), jnp.float32),
            pltpu.VMEM((count, 128), jnp.float32),
            pltpu.SemaphoreType.DMA,
            pltpu.SemaphoreType.DMA,
            pltpu.SemaphoreType.DMA((4,)),
            pltpu.SemaphoreType.DMA((chunks, n_label)),
            pltpu.SemaphoreType.DMA((chunks,)),
            pltpu.SemaphoreType.DMA((3,)),
            pltpu.SemaphoreType.DMA((3, chunks)),
            pltpu.SemaphoreType.DMA,
            pltpu.SemaphoreType.DMA,
        ],
        compiler_params=pltpu.CompilerParams(
            collective_id=0, has_side_effects=True, vmem_limit_bytes=59 * 1024 * 1024),
    )(embeddings, held)
    return updated[None]


def solution(mesh):
    fused = mesh.shape["label"] == 8 and mesh.shape["groups"] == 2
    body = functools.partial(fused_body, mesh.shape["label"]) if fused else plain_body
    return jax.shard_map(
        body,
        mesh=mesh,
        in_specs=(P("label", "groups"), P("cent", ("groups", "label"), None)),
        out_specs=P("cent", ("groups", "label"), None),
        check_vma=False,
    )
```

```python
import functools
import jax
import jax.numpy as jnp
from jax import lax
from jax.experimental import pallas as pl
from jax.experimental.pallas import tpu as pltpu
from jax.sharding import PartitionSpec as P

prior_weight = 1.0
COLS = 2
WIDTHS = (1024, 1024, 768, 768, 768, 768, 768, 768, 768, 768)
PLANE = (1, 3, 5, 7, 9)
COLUMN_LAG = (0, 1, 2, 3)
ACROSS_LAG = (1, 2, 3, 4)
SLOTS = 6
PLAN = {
    (5, 1): (("S", 0),),
    (5, 2): (("J", 0),),
    (6, 1): (("S", 1),),
    (6, 2): (("J", 1),),
    (7, 0): (("K", 0),),
    (7, 1): (("S", 2),),
    (7, 2): (("A", 0), ("J", 2),),
    (8, 0): (("K", 1),),
    (8, 1): (("S", 3),),
    (8, 2): (("A", 1), ("J", 3),),
    (9, 0): (("K", 2),),
    (9, 1): (("S", 4),),
    (9, 2): (("A", 2), ("J", 4),),
    (10, 0): (("K", 3),),
    (10, 1): (("S", 5),),
    (10, 2): (("A", 3), ("J", 5),),
    (11, 0): (("K", 4),),
    (11, 1): (("S", 6),),
    (11, 2): (("A", 4), ("J", 6),),
    (12, 0): (("K", 5),),
    (12, 1): (("S", 7),),
    (12, 2): (("A", 5), ("J", 7),),
    (13, 0): (("K", 6),),
    (13, 1): (("S", 8),),
    (13, 2): (("A", 6), ("J", 8),),
    (13, 3): (("S", 9), ("K", 7), ("K", 8), ("A", 7), ("A", 8), ("A", 9),),
}
MESH = pl.DeviceIdType.MESH


def plain_body(embeddings, centroids):
    held = centroids[0]
    half = embeddings.shape[1] // lax.axis_size("cent")
    mine = lax.dynamic_slice_in_dim(embeddings, lax.axis_index("cent") * half, half, axis=1)
    column = lax.all_gather(mine, "label", axis=0, tiled=True)
    table = lax.all_gather(column, "cent", axis=1, tiled=True)
    half_norms = 0.5 * jnp.sum(jnp.square(held.astype(jnp.float32)), axis=1)
    scores = jnp.dot(held, table, preferred_element_type=jnp.float32) - half_norms[:, None]
    top = jnp.max(scores, axis=0)
    total = jnp.sum(jnp.exp(scores - top[None, :]), axis=0)
    tops = lax.all_gather(jnp.stack([top, total]), ("label", "cent"))
    row_top = jnp.max(tops[:, 0], axis=0)
    row_sum = jnp.sum(tops[:, 1] * jnp.exp(tops[:, 0] - row_top[None]), axis=0)
    weights = (jnp.exp(scores - row_top[None, :]) / row_sum[None, :]).astype(jnp.bfloat16)
    sums = lax.dot_general(weights, table, (((1,), (1,)), ((), ())), preferred_element_type=jnp.float32)
    counts = jnp.sum(weights, axis=1, dtype=jnp.float32)
    updated = (sums + prior_weight * held.astype(jnp.float32)) / (counts + prior_weight)[:, None]
    return updated[None]


def merge(values):
    top = functools.reduce(jnp.maximum, values)
    return top + jnp.log(sum(jnp.exp(value - top) for value in values))


def kernel(n_label, e_ref, c_hbm, out_ref, c_ref, table, expo, tops, stat_core, stat_chip, stat_full, stat_last,
           sums, counts, norms, load_sem, c_sem, send_sem, recv_sem, sib_sem, stat_send, stat_recv):
    rows = e_ref.shape[0]
    labels = table.shape[1]
    chunks = len(WIDTHS)
    starts = [sum(WIDTHS[:j]) for j in range(chunks)]
    n_z = n_label // COLS
    me = lax.axis_index("label")
    core = lax.axis_index("cent")
    z, y = me // COLS, me % COLS
    across_label = z * COLS + 1 - y
    last = chunks - 1
    self_id = me * 2 + core

    def block(index):
        return pl.ds(pl.multiple_of(index * rows, rows), rows)

    def columns(j):
        return pl.ds(starts[j], WIDTHS[j])

    def halves(j):
        return pl.ds(starts[j] // 2, WIDTHS[j] // 2)

    def own_half(j):
        return pl.ds(pl.multiple_of(starts[j] + core * (WIDTHS[j] // 2), 128), WIDTHS[j] // 2)

    load = pltpu.make_async_copy(e_ref, table.at[block(me), :], load_sem)
    load.start()
    c_load = pltpu.make_async_copy(c_hbm, c_ref, c_sem)
    c_load.start()

    barrier = pltpu.get_barrier_semaphore()
    pl.semaphore_signal(barrier, inc=1, device_id={"cent": 1 - core}, device_id_type=MESH)
    pl.semaphore_signal(barrier, inc=1, device_id={"label": across_label}, device_id_type=MESH)

    @pl.when(z < n_z - 1)
    def _():
        pl.semaphore_signal(barrier, inc=1, device_id={"label": me + COLS}, device_id_type=MESH)

    @pl.when(z > 0)
    def _():
        pl.semaphore_signal(barrier, inc=1, device_id={"label": me - COLS}, device_id_type=MESH)

    sums[...] = jnp.zeros_like(sums)
    counts[...] = jnp.zeros_like(counts)
    load.wait()
    pl.semaphore_wait(barrier, 2 + jnp.where(z < n_z - 1, 1, 0) + jnp.where(z > 0, 1, 0))

    def hop(j, index, kind, target):
        part = table.at[block(index), own_half(j)]
        return pltpu.make_async_remote_copy(
            src_ref=part, dst_ref=part, send_sem=send_sem.at[kind],
            recv_sem=recv_sem.at[j, index], device_id={"label": target}, device_id_type=MESH)

    def sibling(j, index, size):
        part = table.at[pl.ds(pl.multiple_of(index * rows, rows), size * rows), own_half(j)]
        return pltpu.make_async_remote_copy(
            src_ref=part, dst_ref=part, send_sem=send_sem.at[3],
            recv_sem=sib_sem.at[j], device_id={"cent": 1 - core}, device_id_type=MESH)

    def up(j, index):
        @pl.when(z < n_z - 1)
        def _():
            hop(j, index, 0, me + COLS).start()

    def down(j, index):
        @pl.when(z > 0)
        def _():
            hop(j, index, 1, me - COLS).start()

    def across(j, index):
        hop(j, index, 2, across_label).start()

    def by_plane(j):
        return j in PLANE

    def relay_own(t):
        if t < chunks:
            up(t, me)
            down(t, me)
            across(t, me)

    def relay_column(t, d):
        j = t - COLUMN_LAG[d]
        if not 0 <= j < chunks:
            return
        for sign in (-1, 1):
            far = z + sign * d
            edge = jnp.logical_or(far == 0, far == n_z - 1)

            @pl.when((far >= 0) & (far < n_z))
            def _():
                index = far * COLS + y
                hop(j, index, 0, me).wait_recv()
                (up if sign < 0 else down)(j, index)
                if by_plane(j):
                    pl.when(jnp.logical_not(edge))(lambda: across(j, index))
                else:
                    across(j, index)

    def relay_across(t, d):
        j = t - ACROSS_LAG[d]
        if not 0 <= j < chunks:
            return
        for sign in ((1,) if d == 0 else (-1, 1)):
            far = z + sign * d

            @pl.when((far >= 0) & (far < n_z))
            def _():
                index = far * COLS + 1 - y
                hop(j, index, 0, me).wait_recv()
                if by_plane(j):
                    pl.when(far == 0)(lambda: up(j, index))
                    pl.when(far == n_z - 1)(lambda: down(j, index))
                if d == 0:
                    sibling(j, index, 1).start()
                else:
                    sibling(j, far * COLS, COLS).start()

    def tell(part, stage, j, target):
        pltpu.make_async_remote_copy(
            src_ref=part, dst_ref=part, send_sem=stat_send.at[stage],
            recv_sem=stat_recv.at[stage, j], device_id=target, device_id_type=MESH).start()

    def hear(part, stage, j):
        pltpu.make_async_copy(part, part, stat_recv.at[stage, j]).wait()

    def score(j):
        width = WIDTHS[j]
        half = width // 2
        others = table.at[pl.ds(0, (n_label - 1) * rows), pl.ds(0, half)]
        pltpu.make_async_copy(others, others, sib_sem.at[j]).wait()
        products = jnp.dot(c_ref[...], table[:, columns(j)], preferred_element_type=jnp.float32)
        scores = products - norms[:, 0:1]
        top = jnp.max(scores, axis=0, keepdims=True)
        exponent = jnp.exp(scores - top)
        expo[j % SLOTS, :, :width] = exponent
        tops[:, columns(j)] = top
        level = top + jnp.log(jnp.sum(exponent, axis=0, keepdims=True))
        if j < last:
            stat_core[core, 0, :, halves(j)] = level[:, :half]
            stat_core[core, 1, :, halves(j)] = level[:, half:]
            tell(stat_core.at[core, 1 - core, :, halves(j)], 0, j, {"cent": 1 - core})
            return
        stat_last[self_id] = level
        for k in range(1, 2 * n_label):
            other = lax.rem(self_id + k, 2 * n_label)
            tell(stat_last.at[self_id], 0, j, {"label": other // 2, "cent": other % 2})

    def join_cores(j):
        hear(stat_core.at[0, 0, :, halves(j)], 0, j)
        stat_chip[me, :, halves(j)] = merge([stat_core[k, core, :, halves(j)] for k in range(2)])
        for k in range(1, n_label):
            tell(stat_chip.at[me, :, halves(j)], 1, j, {"label": lax.rem(me + k, n_label)})

    def join_chips(j):
        hear(stat_chip.at[pl.ds(0, n_label - 1), :, halves(j)], 1, j)
        stat_full[core, :, halves(j)] = merge([stat_chip[k, :, halves(j)] for k in range(n_label)])
        tell(stat_full.at[core, :, halves(j)], 2, j, {"cent": 1 - core})

    def absorb(j):
        width = WIDTHS[j]
        if j < last:
            hear(stat_full.at[0, :, halves(j)], 2, j)
            level = jnp.concatenate([stat_full[k, :, halves(j)] for k in range(2)], axis=1)
        else:
            hear(stat_last.at[pl.ds(0, 2 * n_label - 1)], 0, j)
            level = merge([stat_last[i] for i in range(2 * n_label)])
        factor = jnp.exp(tops[:, columns(j)] - level)
        weights = (expo[j % SLOTS, :, :width] * factor).astype(jnp.bfloat16)
        gained = lax.dot_general(
            weights, table[:, columns(j)], (((1,), (1,)), ((), ())), preferred_element_type=jnp.float32)
        part = counts[...]
        for k in range(width // 128):
            part += weights[:, k * 128:(k + 1) * 128].astype(jnp.float32)
        if j < last:
            sums[...] += gained
            counts[...] = part
        else:
            total = jnp.sum(part, axis=1, keepdims=True)
            held = prior_weight * c_ref[...].astype(jnp.float32)
            out_ref[...] = (sums[...] + gained + held) * (1.0 / (total + prior_weight))

    def relays(t, part):
        if part == 0:
            relay_own(t)
        for d in ((1,), (2,), range(3, n_z))[part]:
            relay_column(t, d)
            relay_across(t, d - 1)
        if part == 2:
            relay_across(t, n_z - 1)

    steps = {"S": score, "J": join_cores, "K": join_chips, "A": absorb}
    for t in range(chunks + ACROSS_LAG[-1]):
        for part in range(4):
            for step, j in PLAN.get((t, part), ()):
                steps[step](j)
            if t == 0 and part == 1:
                c_load.wait()
                centroids = c_ref[...].astype(jnp.float32)
                norms[...] = jnp.broadcast_to(0.5 * jnp.sum(centroids * centroids, axis=1, keepdims=True), norms.shape)
            if part < 3:
                relays(t, part)

    def drain(kind, halves):
        ref = table.at[pl.ds(0, halves * rows // 2), pl.ds(0, labels // 2)]
        pltpu.make_async_copy(ref, ref, send_sem.at[kind]).wait()

    for k in range(n_z):
        @pl.when(z == k)
        def _():
            if k < n_z - 1:
                drain(0, 2 * (k + 1) + 1)
            if k > 0:
                drain(1, 2 * (n_z - k) + 1)
            drain(2, 2 * n_z - (1 if k in (0, n_z - 1) else 2))
    drain(3, 2 * (n_label - 1))
    before = pl.ds(0, (labels - WIDTHS[last]) // 2)
    told = ((stat_core.at[0, 0, :, before], stat_last.at[pl.ds(0, 2 * n_label - 1)]),
            (stat_chip.at[pl.ds(0, n_label - 1), :, before],), (stat_full.at[0, :, before],))
    for stage, parts in enumerate(told):
        for part in parts:
            pltpu.make_async_copy(part, part, stat_send.at[stage]).wait()


def fused_body(n_label, embeddings, centroids):
    held = centroids[0]
    rows, labels = embeddings.shape
    count, depth = held.shape
    if labels != sum(WIDTHS):
        return plain_body(embeddings, centroids)
    chunks = len(WIDTHS)
    updated = pl.pallas_call(
        functools.partial(kernel, n_label),
        out_shape=pltpu.VMEM((count, depth), jnp.float32),
        in_specs=[pl.BlockSpec(memory_space=pl.ANY)] * 2,
        out_specs=pl.BlockSpec(memory_space=pltpu.VMEM),
        scratch_shapes=[
            pltpu.VMEM((count, depth), jnp.bfloat16),
            pltpu.VMEM((depth, labels), jnp.bfloat16),
            pltpu.VMEM((SLOTS, count, max(WIDTHS)), jnp.float32),
            pltpu.VMEM((1, labels), jnp.float32),
            pltpu.VMEM((2, 2, 1, labels // 2), jnp.float32),
            pltpu.VMEM((n_label, 1, labels // 2), jnp.float32),
            pltpu.VMEM((2, 1, labels // 2), jnp.float32),
            pltpu.VMEM((2 * n_label, 1, WIDTHS[-1]), jnp.float32),
            pltpu.VMEM((count, depth), jnp.float32),
            pltpu.VMEM((count, 128), jnp.float32),
            pltpu.VMEM((count, 128), jnp.float32),
            pltpu.SemaphoreType.DMA,
            pltpu.SemaphoreType.DMA,
            pltpu.SemaphoreType.DMA((4,)),
            pltpu.SemaphoreType.DMA((chunks, n_label)),
            pltpu.SemaphoreType.DMA((chunks,)),
            pltpu.SemaphoreType.DMA((3,)),
            pltpu.SemaphoreType.DMA((3, chunks)),
        ],
        compiler_params=pltpu.CompilerParams(
            collective_id=0, has_side_effects=True, vmem_limit_bytes=59 * 1024 * 1024),
    )(embeddings, held)
    return updated[None]


def solution(mesh):
    fused = mesh.shape["label"] == 8 and mesh.shape["groups"] == 2
    body = functools.partial(fused_body, mesh.shape["label"]) if fused else plain_body
    return jax.shard_map(
        body,
        mesh=mesh,
        in_specs=(P("label", "groups"), P("cent", ("groups", "label"), None)),
        out_specs=P("cent", ("groups", "label"), None),
        check_vma=False,
    )
```

```python
import functools
import jax
import jax.numpy as jnp
from jax import lax
from jax.experimental import pallas as pl
from jax.experimental.pallas import tpu as pltpu
from jax.sharding import PartitionSpec as P

prior_weight = 1.0
COLS = 2
WIDTHS = (1024, 1024, 768, 768, 768, 768, 768, 768, 768, 768)
PLANE = (1, 3, 5, 7, 9)
COLUMN_LAG = (0, 1, 2, 3)
ACROSS_LAG = (1, 2, 3, 4)
SLOTS = 6
PLAN = {
    (5, 1): (("S", 0),),
    (5, 2): (("J", 0),),
    (6, 1): (("S", 1),),
    (6, 2): (("J", 1),),
    (7, 0): (("K", 0),),
    (7, 1): (("S", 2),),
    (7, 2): (("A", 0), ("J", 2),),
    (8, 0): (("K", 1),),
    (8, 1): (("S", 3),),
    (8, 2): (("A", 1), ("J", 3),),
    (9, 0): (("K", 2),),
    (9, 1): (("S", 4),),
    (9, 2): (("A", 2), ("J", 4),),
    (10, 0): (("K", 3),),
    (10, 1): (("S", 5),),
    (10, 2): (("A", 3), ("J", 5),),
    (11, 0): (("K", 4),),
    (11, 1): (("S", 6),),
    (11, 2): (("A", 4), ("J", 6),),
    (12, 0): (("K", 5),),
    (12, 1): (("S", 7),),
    (12, 2): (("A", 5), ("J", 7),),
    (13, 0): (("K", 6),),
    (13, 1): (("S", 8),),
    (13, 2): (("A", 6), ("J", 8),),
    (13, 3): (("S", 9), ("K", 7), ("A", 7), ("K", 8), ("A", 8), ("A", 9),),
}
MESH = pl.DeviceIdType.MESH


def plain_body(embeddings, centroids):
    held = centroids[0]
    half = embeddings.shape[1] // lax.axis_size("cent")
    mine = lax.dynamic_slice_in_dim(embeddings, lax.axis_index("cent") * half, half, axis=1)
    column = lax.all_gather(mine, "label", axis=0, tiled=True)
    table = lax.all_gather(column, "cent", axis=1, tiled=True)
    half_norms = 0.5 * jnp.sum(jnp.square(held.astype(jnp.float32)), axis=1)
    scores = jnp.dot(held, table, preferred_element_type=jnp.float32) - half_norms[:, None]
    top = jnp.max(scores, axis=0)
    total = jnp.sum(jnp.exp(scores - top[None, :]), axis=0)
    tops = lax.all_gather(jnp.stack([top, total]), ("label", "cent"))
    row_top = jnp.max(tops[:, 0], axis=0)
    row_sum = jnp.sum(tops[:, 1] * jnp.exp(tops[:, 0] - row_top[None]), axis=0)
    weights = (jnp.exp(scores - row_top[None, :]) / row_sum[None, :]).astype(jnp.bfloat16)
    sums = lax.dot_general(weights, table, (((1,), (1,)), ((), ())), preferred_element_type=jnp.float32)
    counts = jnp.sum(weights, axis=1, dtype=jnp.float32)
    updated = (sums + prior_weight * held.astype(jnp.float32)) / (counts + prior_weight)[:, None]
    return updated[None]


def merge(values):
    top = functools.reduce(jnp.maximum, values)
    return top + jnp.log(sum(jnp.exp(value - top) for value in values))


def kernel(n_label, e_ref, c_hbm, out_ref, c_ref, table, expo, tops, stat_core, stat_chip, stat_full, stat_last,
           sums, counts, norms, load_sem, c_sem, send_sem, recv_sem, sib_sem, stat_send, stat_recv):
    rows = e_ref.shape[0]
    labels = table.shape[1]
    chunks = len(WIDTHS)
    starts = [sum(WIDTHS[:j]) for j in range(chunks)]
    n_z = n_label // COLS
    me = lax.axis_index("label")
    core = lax.axis_index("cent")
    z, y = me // COLS, me % COLS
    across_label = z * COLS + 1 - y
    last = chunks - 1
    self_id = me * 2 + core

    def block(index):
        return pl.ds(pl.multiple_of(index * rows, rows), rows)

    def columns(j):
        return pl.ds(starts[j], WIDTHS[j])

    def halves(j):
        return pl.ds(starts[j] // 2, WIDTHS[j] // 2)

    def own_half(j):
        return pl.ds(pl.multiple_of(starts[j] + core * (WIDTHS[j] // 2), 128), WIDTHS[j] // 2)

    load = pltpu.make_async_copy(e_ref, table.at[block(me), :], load_sem)
    load.start()
    c_load = pltpu.make_async_copy(c_hbm, c_ref, c_sem)
    c_load.start()

    barrier = pltpu.get_barrier_semaphore()
    pl.semaphore_signal(barrier, inc=1, device_id={"cent": 1 - core}, device_id_type=MESH)
    pl.semaphore_signal(barrier, inc=1, device_id={"label": across_label}, device_id_type=MESH)

    @pl.when(z < n_z - 1)
    def _():
        pl.semaphore_signal(barrier, inc=1, device_id={"label": me + COLS}, device_id_type=MESH)

    @pl.when(z > 0)
    def _():
        pl.semaphore_signal(barrier, inc=1, device_id={"label": me - COLS}, device_id_type=MESH)

    sums[...] = jnp.zeros_like(sums)
    counts[...] = jnp.zeros_like(counts)
    load.wait()
    pl.semaphore_wait(barrier, 2 + jnp.where(z < n_z - 1, 1, 0) + jnp.where(z > 0, 1, 0))

    def hop(j, index, kind, target):
        part = table.at[block(index), own_half(j)]
        return pltpu.make_async_remote_copy(
            src_ref=part, dst_ref=part, send_sem=send_sem.at[kind],
            recv_sem=recv_sem.at[j, index], device_id={"label": target}, device_id_type=MESH)

    def sibling(j, index, size):
        part = table.at[pl.ds(pl.multiple_of(index * rows, rows), size * rows), own_half(j)]
        return pltpu.make_async_remote_copy(
            src_ref=part, dst_ref=part, send_sem=send_sem.at[3],
            recv_sem=sib_sem.at[j], device_id={"cent": 1 - core}, device_id_type=MESH)

    def up(j, index):
        @pl.when(z < n_z - 1)
        def _():
            hop(j, index, 0, me + COLS).start()

    def down(j, index):
        @pl.when(z > 0)
        def _():
            hop(j, index, 1, me - COLS).start()

    def across(j, index):
        hop(j, index, 2, across_label).start()

    def by_plane(j):
        return j in PLANE

    def relay_own(t):
        if t < chunks:
            up(t, me)
            down(t, me)
            across(t, me)

    def relay_column(t, d):
        j = t - COLUMN_LAG[d]
        if not 0 <= j < chunks:
            return
        for sign in (-1, 1):
            far = z + sign * d
            edge = jnp.logical_or(far == 0, far == n_z - 1)

            @pl.when((far >= 0) & (far < n_z))
            def _():
                index = far * COLS + y
                hop(j, index, 0, me).wait_recv()
                if by_plane(j):
                    pl.when(jnp.logical_not(edge))(lambda: across(j, index))
                else:
                    across(j, index)
                (up if sign < 0 else down)(j, index)

    def relay_across(t, d):
        j = t - ACROSS_LAG[d]
        if not 0 <= j < chunks:
            return
        for sign in ((1,) if d == 0 else (-1, 1)):
            far = z + sign * d

            @pl.when((far >= 0) & (far < n_z))
            def _():
                index = far * COLS + 1 - y
                hop(j, index, 0, me).wait_recv()
                if by_plane(j):
                    pl.when(far == 0)(lambda: up(j, index))
                    pl.when(far == n_z - 1)(lambda: down(j, index))
                if d == 0:
                    sibling(j, index, 1).start()
                else:
                    sibling(j, far * COLS, COLS).start()

    def tell(part, stage, j, target):
        pltpu.make_async_remote_copy(
            src_ref=part, dst_ref=part, send_sem=stat_send.at[stage],
            recv_sem=stat_recv.at[stage, j], device_id=target, device_id_type=MESH).start()

    def hear(part, stage, j):
        pltpu.make_async_copy(part, part, stat_recv.at[stage, j]).wait()

    def score(j):
        width = WIDTHS[j]
        half = width // 2
        others = table.at[pl.ds(0, (n_label - 1) * rows), pl.ds(0, half)]
        pltpu.make_async_copy(others, others, sib_sem.at[j]).wait()
        products = jnp.dot(c_ref[...], table[:, columns(j)], preferred_element_type=jnp.float32)
        scores = products - norms[:, 0:1]
        top = jnp.max(scores, axis=0, keepdims=True)
        exponent = jnp.exp(scores - top)
        expo[j % SLOTS, :, :width] = exponent
        tops[:, columns(j)] = top
        level = top + jnp.log(jnp.sum(exponent, axis=0, keepdims=True))
        if j < last:
            stat_core[core, 0, :, halves(j)] = level[:, :half]
            stat_core[core, 1, :, halves(j)] = level[:, half:]
            tell(stat_core.at[core, 1 - core, :, halves(j)], 0, j, {"cent": 1 - core})
            return
        stat_last[self_id] = level
        for k in range(1, 2 * n_label):
            other = lax.rem(self_id + k, 2 * n_label)
            tell(stat_last.at[self_id], 0, j, {"label": other // 2, "cent": other % 2})

    def join_cores(j):
        hear(stat_core.at[0, 0, :, halves(j)], 0, j)
        stat_chip[me, :, halves(j)] = merge([stat_core[k, core, :, halves(j)] for k in range(2)])
        for k in range(1, n_label):
            tell(stat_chip.at[me, :, halves(j)], 1, j, {"label": lax.rem(me + k, n_label)})

    def join_chips(j):
        hear(stat_chip.at[pl.ds(0, n_label - 1), :, halves(j)], 1, j)
        stat_full[core, :, halves(j)] = merge([stat_chip[k, :, halves(j)] for k in range(n_label)])
        tell(stat_full.at[core, :, halves(j)], 2, j, {"cent": 1 - core})

    def absorb(j):
        width = WIDTHS[j]
        if j < last:
            hear(stat_full.at[0, :, halves(j)], 2, j)
            level = jnp.concatenate([stat_full[k, :, halves(j)] for k in range(2)], axis=1)
        else:
            hear(stat_last.at[pl.ds(0, 2 * n_label - 1)], 0, j)
            level = merge([stat_last[i] for i in range(2 * n_label)])
        factor = jnp.exp(tops[:, columns(j)] - level)
        weights = (expo[j % SLOTS, :, :width] * factor).astype(jnp.bfloat16)
        gained = lax.dot_general(
            weights, table[:, columns(j)], (((1,), (1,)), ((), ())), preferred_element_type=jnp.float32)
        part = counts[...]
        for k in range(width // 128):
            part += weights[:, k * 128:(k + 1) * 128].astype(jnp.float32)
        if j < last:
            sums[...] += gained
            counts[...] = part
        else:
            total = jnp.sum(part, axis=1, keepdims=True)
            held = prior_weight * c_ref[...].astype(jnp.float32)
            out_ref[...] = (sums[...] + gained + held) * (1.0 / (total + prior_weight))

    def relays(t, part):
        if part == 0:
            relay_own(t)
        for d in ((1,), (2,), range(3, n_z))[part]:
            relay_column(t, d)
            relay_across(t, d - 1)
        if part == 2:
            relay_across(t, n_z - 1)

    steps = {"S": score, "J": join_cores, "K": join_chips, "A": absorb}
    for t in range(chunks + ACROSS_LAG[-1]):
        for part in range(4):
            for step, j in PLAN.get((t, part), ()):
                steps[step](j)
            if t == 0 and part == 1:
                c_load.wait()
                centroids = c_ref[...].astype(jnp.float32)
                norms[...] = jnp.broadcast_to(0.5 * jnp.sum(centroids * centroids, axis=1, keepdims=True), norms.shape)
            if part < 3:
                relays(t, part)

    def drain(kind, halves):
        ref = table.at[pl.ds(0, halves * rows // 2), pl.ds(0, labels // 2)]
        pltpu.make_async_copy(ref, ref, send_sem.at[kind]).wait()

    for k in range(n_z):
        @pl.when(z == k)
        def _():
            if k < n_z - 1:
                drain(0, 2 * (k + 1) + 1)
            if k > 0:
                drain(1, 2 * (n_z - k) + 1)
            drain(2, 2 * n_z - (1 if k in (0, n_z - 1) else 2))
    drain(3, 2 * (n_label - 1))
    before = pl.ds(0, (labels - WIDTHS[last]) // 2)
    told = ((stat_core.at[0, 0, :, before], stat_last.at[pl.ds(0, 2 * n_label - 1)]),
            (stat_chip.at[pl.ds(0, n_label - 1), :, before],), (stat_full.at[0, :, before],))
    for stage, parts in enumerate(told):
        for part in parts:
            pltpu.make_async_copy(part, part, stat_send.at[stage]).wait()


def fused_body(n_label, embeddings, centroids):
    held = centroids[0]
    rows, labels = embeddings.shape
    count, depth = held.shape
    if labels != sum(WIDTHS):
        return plain_body(embeddings, centroids)
    chunks = len(WIDTHS)
    updated = pl.pallas_call(
        functools.partial(kernel, n_label),
        out_shape=pltpu.VMEM((count, depth), jnp.float32),
        in_specs=[pl.BlockSpec(memory_space=pl.ANY)] * 2,
        out_specs=pl.BlockSpec(memory_space=pltpu.VMEM),
        scratch_shapes=[
            pltpu.VMEM((count, depth), jnp.bfloat16),
            pltpu.VMEM((depth, labels), jnp.bfloat16),
            pltpu.VMEM((SLOTS, count, max(WIDTHS)), jnp.float32),
            pltpu.VMEM((1, labels), jnp.float32),
            pltpu.VMEM((2, 2, 1, labels // 2), jnp.float32),
            pltpu.VMEM((n_label, 1, labels // 2), jnp.float32),
            pltpu.VMEM((2, 1, labels // 2), jnp.float32),
            pltpu.VMEM((2 * n_label, 1, WIDTHS[-1]), jnp.float32),
            pltpu.VMEM((count, depth), jnp.float32),
            pltpu.VMEM((count, 128), jnp.float32),
            pltpu.VMEM((count, 128), jnp.float32),
            pltpu.SemaphoreType.DMA,
            pltpu.SemaphoreType.DMA,
            pltpu.SemaphoreType.DMA((4,)),
            pltpu.SemaphoreType.DMA((chunks, n_label)),
            pltpu.SemaphoreType.DMA((chunks,)),
            pltpu.SemaphoreType.DMA((3,)),
            pltpu.SemaphoreType.DMA((3, chunks)),
        ],
        compiler_params=pltpu.CompilerParams(
            collective_id=0, has_side_effects=True, vmem_limit_bytes=59 * 1024 * 1024),
    )(embeddings, held)
    return updated[None]


def solution(mesh):
    fused = mesh.shape["label"] == 8 and mesh.shape["groups"] == 2
    body = functools.partial(fused_body, mesh.shape["label"]) if fused else plain_body
    return jax.shard_map(
        body,
        mesh=mesh,
        in_specs=(P("label", "groups"), P("cent", ("groups", "label"), None)),
        out_specs=P("cent", ("groups", "label"), None),
        check_vma=False,
    )
```
